32 devices in a mesh: groups: 2 (over y), seq: 4 (over z), head: 2 (over x), batch: 2 (over core).
Axes of the slice: x: 2, y: 2, z: 4, core: 2. Of those that a mesh axis runs over, the one named last changes fastest.
Arguments:
- x_values: bfloat16 [4, 1024, 8192], P(('groups', 'batch'), 'seq', 'head'), parts along dimension 0, may hold values from -6 to 6
- z_gate: bfloat16 [4, 1024, 8192], P(('groups', 'batch'), 'seq', 'head'), parts along dimension 0, may hold values from -6 to 6
- write_basis: bfloat16 [4, 1024, 1024], P(('groups', 'batch'), 'seq', 'head'), parts along dimension 0, may hold values from -6 to 6
- read_basis: bfloat16 [4, 1024, 1024], P(('groups', 'batch'), 'seq', 'head'), parts along dimension 0, may hold values from -0.5 to 0.5
- step_size: float32 [4, 1024, 128], P(('groups', 'batch'), 'seq', 'head'), parts along dimension 0, may hold values from 0.5 to 2
- log_decay: float32 [4, 1024, 128], P(('groups', 'batch'), 'seq', 'head'), parts along dimension 0, may hold values from -0.8 to 0
- cached_states: bfloat16 [4, 4, 128, 64, 128], P(('groups', 'batch'), None, 'head', 'seq'), parts along dimension 0, may hold values from -96 to 96
- session_slots: int32 [4, 4], P(('groups', 'batch')), parts along dimension 0, may hold values from 0 to 3, each once within a row
- conv_lengths: int32 [4, 4], P(('groups', 'batch')), parts along dimension 0, may hold values from 1 to 4, 8 in all within a row
- norm_gain: float32 [8192], P('head'), may hold values from 0.1 to 1.9
- out_weight: bfloat16 [8192, 4096], P('head', 'seq'), may hold values from -0.0625 to 0.0625
Outputs:
- layer_out: bfloat16 [4, 1024, 4096], P(('groups', 'batch'), 'seq', 'head'), parts along dimension 0
The draws below stay inside these ranges and needn't reach their ends.
There are 2 independent parts, one for each index of `groups`. The reference program is written for one: setup_inputs(seed, part) draws one part's arguments, and reference() takes and returns one part's arrays. A program takes and returns all parts, laid end to end along the dimension named above; an argument that names none is the same for every part. Nothing has to cross between parts.
Inputs may be any that keep to these rules, and one draw needn't show every extreme that they name: `session_slots`: each row's entries name every pool entry once. `conv_lengths`: each row's lengths sum to 8.
All inputs are finite; a program needn't handle non-finite values.
Results may differ from the reference program's by a relative error of at most 0.017.
Values may be sent and summed in bfloat16 or wider, within the bound.
A program may use at most 128 MiB of HBM per device.

```python
import math
import jax
import jax.numpy as jnp
import numpy as np
from jax import lax

D = 4096
HEADS = 128
HEAD_DIM = 64
STATE = 128
GROUPS = 8
STRETCH = 128
CONVS = 4
BUNDLED_LINES = 2
LINE_SLOTS = 1024
STRETCHES_ROW = 8
MOST_STRETCHES = 4
N_HEAD = 2


def draw_log_decay(key, part):
    sampler_seeds = jax.random.split(key, 4)
    fading_speeds = jnp.exp(jax.random.uniform(sampler_seeds[0], (HEADS,), jnp.float32, math.log(0.5 / LINE_SLOTS), math.log(1.0 / 30.0)))
    shrink_multiplier = jnp.exp(jax.random.uniform(sampler_seeds[1], (BUNDLED_LINES, LINE_SLOTS, HEADS), jnp.float32, math.log(0.5), math.log(2.0)))
    word_spurts = jax.random.uniform(sampler_seeds[2], (BUNDLED_LINES, LINE_SLOTS, 1), jnp.float32) < 3.0 / LINE_SLOTS
    incoming_quantity = jax.random.uniform(sampler_seeds[3], (BUNDLED_LINES, LINE_SLOTS, HEADS), jnp.float32, 0.22, 0.69)
    return -(fading_speeds[None, None, :] * shrink_multiplier + jnp.where(word_spurts, incoming_quantity, 0.0))


def steps_of(stream_key, shape, pieces, low, high):
    factor_of, own = 1.0, jax.random.fold_in(stream_key, 6)
    for dim, blocks in pieces:
        steps = jnp.exp(jax.random.uniform(jax.random.fold_in(own, dim), (blocks,), jnp.float32, low / len(pieces), high / len(pieces)))
        factor_of = factor_of * jnp.repeat(steps, shape[dim] // blocks).reshape([-1 if axis == dim else 1 for axis in range(len(shape))])
    return factor_of


def length_profile(number_of, total, limit, slope):
    loads = [(1 << 20) // math.isqrt(standing ** slope) + 1 for standing in range(2, number_of + 1)]
    surplus, counts = total - limit - (number_of - 1), [1] * (number_of - 1)
    while surplus > 0:
        free = [i for i in range(number_of - 1) if counts[i] < limit]
        whole, budget = sum([loads[i] for i in free]), surplus
        for i in free:
            extra = min(limit - counts[i], max(1, budget * loads[i] // whole), surplus)
            counts[i] = counts[i] + extra
            surplus = surplus - extra
    return np.array([limit] + counts)


def uneven_parts(rng, number_of, total, most, lean):
    if number_of == 2:
        one = jax.random.randint(rng, (), max(1, total - most), min(most, total - 1) + 1)
        return jnp.stack([one, total - one])
    sizes = jnp.asarray(length_profile(number_of, total, most, lean), jnp.int32)
    twos = (number_of - 1) // 2
    source_of, sink = sizes[1:1 + 2 * twos:2], sizes[2:2 + 2 * twos:2]
    margin = jnp.minimum(source_of - 1, most - sink)
    shifted = jax.random.randint(jax.random.fold_in(rng, 1), (twos,), 0, 1 << 20) % (margin + 1)
    sizes = sizes.at[1:1 + 2 * twos:2].set(source_of - shifted).at[2:2 + 2 * twos:2].set(sink + shifted)
    return sizes[jax.random.permutation(jax.random.fold_in(rng, 2), number_of)]


def scatter_about(rng, dims, scale, limit, cuts=(), kind=jnp.bfloat16):
    factor_of = steps_of(rng, dims, cuts, -0.22, 0.18) if cuts else 1.0
    drawn = jax.random.normal(rng, dims, jnp.float32) * scale * factor_of
    return jnp.minimum(jnp.maximum(drawn, -limit), limit).astype(kind)


def setup_inputs(seed: int = 0, part: int = 0) -> dict:
    streams_of = jax.random.split(jax.random.key(seed), 12)
    part_splits = jax.random.split(jax.random.fold_in(streams_of[11], part), 12)
    x_values = scatter_about(part_splits[0], (BUNDLED_LINES, LINE_SLOTS, HEADS * HEAD_DIM), 1.0, 6.0, ((0, 2), (1, 4), (2, 2)))
    z_gate = scatter_about(part_splits[1], (BUNDLED_LINES, LINE_SLOTS, HEADS * HEAD_DIM), 1.0, 6.0, ((0, 2), (1, 4), (2, 2)))
    write_basis = scatter_about(part_splits[2], (BUNDLED_LINES, LINE_SLOTS, GROUPS * STATE), 1.0, 6.0, ((0, 2), (1, 4), (2, 2)))
    read_basis = scatter_about(part_splits[3], (BUNDLED_LINES, LINE_SLOTS, GROUPS * STATE), STATE ** -0.5, 0.5, ((0, 2), (1, 4), (2, 2)))
    step_size = jnp.clip(jnp.exp(math.log(2.0) - 1.3862944 * jax.random.uniform(part_splits[4], (BUNDLED_LINES, LINE_SLOTS, HEADS), jnp.float32) ** steps_of(part_splits[4], (BUNDLED_LINES, LINE_SLOTS, HEADS), ((0, 2), (1, 4), (2, 2)), -0.2, 0.2)), 0.5, 2.0)
    log_decay = draw_log_decay(jax.random.fold_in(jax.random.fold_in(streams_of[11], part), 71), part)
    cached_states = scatter_about(part_splits[6], (BUNDLED_LINES, CONVS, HEADS, HEAD_DIM, STATE), 16.0, 96.0, ((0, 2), (2, 2), (3, 4)))
    session_slots = jax.vmap(lambda own: jax.random.permutation(own, CONVS))(jax.random.split(part_splits[7], BUNDLED_LINES)).reshape((BUNDLED_LINES, CONVS)).astype(jnp.int32)
    conv_lengths = jax.vmap(lambda own: uneven_parts(own, CONVS, STRETCHES_ROW, MOST_STRETCHES, 2))(jax.random.split(part_splits[8], BUNDLED_LINES)).reshape((BUNDLED_LINES, CONVS)).astype(jnp.int32)
    norm_gain = jnp.clip(1.0 + 0.18 * jax.random.normal(streams_of[9], (HEADS * HEAD_DIM,), jnp.float32), 0.1, 1.9)
    out_weight = scatter_about(streams_of[10], (HEADS * HEAD_DIM, D), (HEADS * HEAD_DIM) ** -0.5, 0.0625, ((0, 2), (1, 4)))
    return {"x_values": x_values, "z_gate": z_gate, "write_basis": write_basis, "read_basis": read_basis, "step_size": step_size, "log_decay": log_decay, "cached_states": cached_states, "session_slots": session_slots, "conv_lengths": conv_lengths, "norm_gain": norm_gain, "out_weight": out_weight}


def row_states(x_row, write_row, read_row, step_row, decay_row, cached_row, slots_row, lengths_row):
    per_group = HEADS // GROUPS
    blocks = LINE_SLOTS // STRETCH
    begins = (jnp.cumsum(lengths_row) - lengths_row).astype(jnp.int32)
    block_ids = jnp.arange(blocks, dtype=jnp.int32)
    flags = jnp.any(begins[None, :] == block_ids[:, None], axis=1)
    owners = lax.optimization_barrier(jnp.sum((begins[None, :] <= block_ids[:, None]).astype(jnp.int32), axis=1)) - 1
    convs = jnp.arange(CONVS, dtype=jnp.int32)
    slot_ids = lax.optimization_barrier(jnp.sum(jnp.where(convs[None, :] == owners[:, None], slots_row[None, :], 0), axis=1)).astype(jnp.int32)
    values = x_row.reshape(blocks, STRETCH, HEADS, HEAD_DIM)
    writes = write_row.reshape(blocks, STRETCH, GROUPS, STATE)
    reads = read_row.reshape(blocks, STRETCH, GROUPS, STATE)
    steps_b = step_row.reshape(blocks, STRETCH, HEADS)
    logs = decay_row.reshape(blocks, STRETCH, HEADS)
    lower = jnp.arange(STRETCH)[:, None] >= jnp.arange(STRETCH)[None, :]

    def advance(state_now, item):
        value_b, write_b, read_b, step_b, log_b, flag, slot = item
        prior = lax.dynamic_index_in_dim(cached_row, slot, 0, keepdims=False).astype(jnp.float32)
        state_now = jnp.where(flag, prior, state_now)
        running = jnp.cumsum(log_b, axis=0)
        by_head = running.T
        spread = by_head[:, :, None] - by_head[:, None, :]
        fading = jnp.where(lower, jnp.exp(jnp.where(lower, spread, 0.0)), 0.0)
        scores = jnp.einsum('ign,jgn->gij', read_b.astype(jnp.float32), write_b.astype(jnp.float32))
        scores = jnp.repeat(scores, per_group, axis=0)
        mixing = (scores * fading * step_b.T[:, None, :]).astype(jnp.bfloat16)
        inner = jnp.einsum('hij,jhp->ihp', mixing.astype(jnp.float32), value_b.astype(jnp.float32))
        read_heads = jnp.repeat(read_b, per_group, axis=1).astype(jnp.float32)
        inflow = jnp.exp(running)[:, :, None] * jnp.einsum('ihn,hpn->ihp', read_heads, state_now, precision=lax.Precision.HIGHEST)
        write_heads = jnp.repeat(write_b, per_group, axis=1).astype(jnp.float32)
        to_end = jnp.exp(running[-1][None, :] - running) * step_b
        weighted = (write_heads * to_end[:, :, None]).astype(jnp.bfloat16)
        stretch_state = jnp.einsum('jhp,jhn->hpn', value_b.astype(jnp.float32), weighted.astype(jnp.float32))
        state_next = jnp.exp(running[-1])[:, None, None] * state_now + stretch_state
        return (state_next, inner + inflow)
    start_state = jnp.zeros((HEADS, HEAD_DIM, STATE), jnp.float32)
    unused, mixed = lax.scan(advance, start_state, (values, writes, reads, steps_b, logs, flags, slot_ids))
    return mixed.reshape(LINE_SLOTS, HEADS * HEAD_DIM)

def reference(x_values, z_gate, write_basis, read_basis, step_size, log_decay, cached_states, session_slots, conv_lengths, norm_gain, out_weight):
    outputs = []
    block_width = HEADS * HEAD_DIM // N_HEAD
    for row in range(BUNDLED_LINES):
        mixed = row_states(x_values[row], write_basis[row], read_basis[row], step_size[row], log_decay[row], cached_states[row], session_slots[row], conv_lengths[row])
        gated = mixed * jax.nn.silu(z_gate[row].astype(jnp.float32))
        grouped = gated.reshape(LINE_SLOTS, GROUPS, -1)
        scaled = grouped * lax.rsqrt(lax.optimization_barrier(jnp.mean(grouped * grouped, axis=2, keepdims=True)) + 1e-05)
        normed = (scaled.reshape(LINE_SLOTS, HEADS * HEAD_DIM) * norm_gain).astype(jnp.bfloat16)
        total = jnp.zeros((LINE_SLOTS, D), jnp.float32)
        for block in range(N_HEAD):
            partial_value = jnp.dot(normed[:, block * block_width:(block + 1) * block_width], out_weight[block * block_width:(block + 1) * block_width], preferred_element_type=jnp.float32)
            rounded = lax.optimization_barrier(partial_value.astype(jnp.bfloat16))
            total = total + rounded.astype(jnp.float32)
        outputs.append(total.astype(jnp.bfloat16))
    return jnp.stack(outputs)
```

```python
import functools

import jax
import jax.numpy as jnp
from jax import lax
from jax.sharding import PartitionSpec as P

HEAD_DIM = 64
STATE = 128
STRETCH = 128


def prefix(value, axis, join, neutral):
    place = lax.axis_index(axis)
    gathered = jax.tree.map(
        lambda a, kind: lax.all_gather(a.astype(kind), axis), value, (jnp.bfloat16, jnp.bfloat16)
    )
    state = jax.tree.map(lambda a, e: jnp.zeros_like(a) + jnp.asarray(e, a.dtype), value, neutral)

    def one(step, state):
        return join(
            state,
            jax.tree.map(
                lambda a, own: lax.dynamic_index_in_dim(a, step, 0, False).astype(own.dtype),
                gathered,
                value,
            ),
        )

    return lax.fori_loop(0, place, one, state)


def combine_pair(earlier, later):
    gain_a, state_a = earlier
    gain_b, state_b = later
    return (gain_a * gain_b, gain_b[:, None, None] * state_a + state_b)


def run_blocks(state_in, priors, flags, totals, block_states):
    running = state_in
    entering = []
    for number in range(flags.shape[0]):
        running = jnp.where(flags[number], priors[number], running)
        entering.append(running)
        running = totals[number][:, None, None] * running + block_states[number]
    return (jnp.stack(entering), running)


def nearest_first(place, count):
    return sorted(range(count), key=lambda j: (abs(j - place), j))


def fetch_weights(out_weight):
    count = lax.axis_size("seq")
    place = lax.axis_index("seq")
    halves = lax.axis_size("groups")
    part_cols = out_weight.shape[1] // lax.axis_size("batch")
    part_rows = out_weight.shape[0] // halves
    col = lax.axis_index("batch") * part_cols
    row = lax.axis_index("groups") * part_rows
    own = lax.dynamic_slice_in_dim(out_weight, col, part_cols, 1)
    own_half = lax.dynamic_slice(out_weight, (row, col), (part_rows, part_cols))
    up_pairs = [(i, i + 1) for i in range(count - 1)]
    down_pairs = [(i + 1, i) for i in range(count - 1)]
    moved = {}
    up = down = own_half
    for step in range(1, count):
        up = lax.ppermute(up, "seq", up_pairs)
        down = lax.ppermute(down, "seq", down_pairs)
        moved[-step] = up
        moved[step] = down
    arrivals = []
    for rank in range(1, count):
        chosen = None
        for offset in sorted(moved):
            places = [p for p in range(count) if nearest_first(p, count)[rank] - p == offset]
            if not places:
                continue
            if chosen is None:
                chosen = moved[offset]
                continue
            here = functools.reduce(jnp.logical_or, [place == p for p in places])
            chosen = jnp.where(here, moved[offset], chosen)
        other = [
            lax.ppermute(chosen, "groups", [(i, (i + turn) % halves) for i in range(halves)])
            for turn in range(1, halves)
        ]
        arrivals.append([chosen] + other)
    return own, own_half, arrivals


def project(both_rows, own, own_half, arrivals, tokens):
    count = lax.axis_size("seq")
    place = lax.axis_index("seq")
    halves = lax.axis_size("groups")
    mine = lax.axis_index("groups")
    part_rows, part_cols = own_half.shape
    strips = [
        lax.dynamic_slice_in_dim(
            both_rows, lax.rem(mine - turn + halves, halves) * part_rows, part_rows, 1
        )
        for turn in range(halves)
    ]
    order = jnp.array([nearest_first(p, count) for p in range(count)], jnp.int32)[place]
    slots = jnp.zeros((count, both_rows.shape[0], part_cols), jnp.bfloat16)
    dot = functools.partial(jnp.dot, preferred_element_type=jnp.float32)
    for rank in range(count):
        if rank == 0:
            total = dot(both_rows, own)
        else:
            total = sum(dot(strip, piece) for strip, piece in zip(strips, arrivals[rank - 1]))
        slots = lax.dynamic_update_index_in_dim(slots, total.astype(jnp.bfloat16), order[rank], 0)
    summed = lax.psum_scatter(slots, "head", scatter_dimension=0, tiled=True)
    spans = summed.shape[0]
    pairs = lax.axis_size("batch")
    sections = summed.reshape(spans, pairs, tokens, part_cols)
    regrouped = lax.all_to_all(sections, "batch", split_axis=1, concat_axis=1, tiled=True)
    return jnp.transpose(regrouped, (2, 0, 1, 3)).reshape(1, tokens, spans * pairs * part_cols)


def body(
    x_values,
    z_gate,
    write_basis,
    read_basis,
    step_size,
    log_decay,
    cached_states,
    session_slots,
    conv_lengths,
    norm_gain,
    out_weight,
):
    own, own_half, arrivals = fetch_weights(out_weight)
    tokens = x_values.shape[1]
    width = x_values.shape[2]
    heads_dev = step_size.shape[2]
    groups_dev = write_basis.shape[2] // STATE
    per_group = heads_dev // groups_dev
    blocks = tokens // STRETCH
    seq_index = lax.axis_index("seq")
    block_ids = seq_index * blocks + jnp.arange(blocks, dtype=jnp.int32)
    lengths_row = conv_lengths[0]
    begins = jnp.cumsum(lengths_row) - lengths_row
    flags = jnp.any(begins[None, :] == block_ids[:, None], axis=1)
    owners = jnp.sum((begins[None, :] <= block_ids[:, None]).astype(jnp.int32), axis=1) - 1
    convs = jnp.arange(lengths_row.shape[0], dtype=jnp.int32)
    slot_ids = jnp.sum(
        jnp.where(convs[None, :] == owners[:, None], session_slots[0][None, :], 0), axis=1
    )
    picker = (convs[None, :] == slot_ids[:, None]).astype(jnp.bfloat16)
    chosen = jnp.einsum(
        "kc,chpn->khpn",
        picker,
        lax.all_gather(cached_states, "seq", axis=3, tiled=True)[0],
        preferred_element_type=jnp.float32,
    )
    values = x_values[0].reshape(blocks, STRETCH, heads_dev, HEAD_DIM)
    writes = write_basis[0].reshape(blocks, STRETCH, groups_dev, STATE)
    reads = read_basis[0].reshape(blocks, STRETCH, groups_dev, STATE)
    steps_b = step_size[0].reshape(blocks, STRETCH, heads_dev)
    logs = log_decay[0].reshape(blocks, STRETCH, heads_dev)
    running_log = jnp.cumsum(logs, axis=1)
    by_head = jnp.transpose(running_log, (0, 2, 1))
    lower = jnp.arange(STRETCH)[:, None] >= jnp.arange(STRETCH)[None, :]
    spread = by_head[:, :, :, None] - by_head[:, :, None, :]
    fading = jnp.where(lower, jnp.exp(jnp.where(lower, spread, 0.0)), 0.0)
    scores = jnp.einsum("cign,cjgn->cgij", reads, writes, preferred_element_type=jnp.float32)
    scores = jnp.repeat(scores, per_group, axis=1)
    mixing = (scores * fading * jnp.transpose(steps_b, (0, 2, 1))[:, :, None, :]).astype(
        jnp.bfloat16
    )
    inner = jnp.einsum("chij,cjhp->cihp", mixing, values, preferred_element_type=jnp.float32)
    to_end = jnp.exp(running_log[:, -1:, :] - running_log) * steps_b
    write_heads = jnp.repeat(writes, per_group, axis=2)
    weighted = (write_heads.astype(jnp.float32) * to_end[:, :, :, None]).astype(jnp.bfloat16)
    block_states = jnp.einsum(
        "cjhp,cjhn->chpn", values, weighted, preferred_element_type=jnp.float32
    )
    totals = jnp.exp(running_log[:, -1, :])
    whole_gain = jnp.prod(totals, axis=0) * (1.0 - jnp.any(flags).astype(jnp.float32))
    zero_state = jnp.zeros((heads_dev, HEAD_DIM, STATE), jnp.float32)
    ones_head = jnp.ones((heads_dev,), jnp.float32)
    unused, device_state = run_blocks(zero_state, chosen, flags, totals, block_states)
    gain_in, state_in = prefix(
        (whole_gain, device_state), "seq", combine_pair, (ones_head, zero_state)
    )
    entering, unused_end = run_blocks(state_in, chosen, flags, totals, block_states)
    read_heads = jnp.repeat(reads, per_group, axis=2).astype(jnp.float32)
    inflow = jnp.exp(running_log)[:, :, :, None] * jnp.einsum(
        "cihn,chpn->cihp", read_heads, entering, precision=lax.Precision.HIGHEST
    )
    mixed = (inner + inflow).reshape(tokens, width)
    gated = mixed * jax.nn.silu(z_gate[0].astype(jnp.float32))
    grouped = gated.reshape(tokens, groups_dev, -1)
    scaled = grouped * lax.rsqrt(jnp.mean(grouped * grouped, axis=2, keepdims=True) + 1e-05)
    normed = (scaled.reshape(tokens, width) * norm_gain).astype(jnp.bfloat16)
    both_rows = lax.all_gather(normed, "batch", axis=0, tiled=True)
    return project(both_rows, own, own_half, arrivals, tokens)


def solution(mesh):
    placed = (
        P(("groups", "batch"), "seq", "head"),
        P(("groups", "batch"), "seq", "head"),
        P(("groups", "batch"), "seq", "head"),
        P(("groups", "batch"), "seq", "head"),
        P(("groups", "batch"), "seq", "head"),
        P(("groups", "batch"), "seq", "head"),
        P(("groups", "batch"), None, "head", "seq", None),
        P(("groups", "batch"), None),
        P(("groups", "batch"), None),
        P("head"),
        P("head", "seq"),
    )
    return jax.shard_map(
        body,
        mesh=mesh,
        in_specs=placed,
        out_specs=P(("groups", "batch"), "seq", "head"),
        check_vma=False,
    )
```

```python
import functools

import jax
import jax.numpy as jnp
from jax import lax
from jax.sharding import PartitionSpec as P

HEAD_DIM = 64
STATE = 128
STRETCH = 128


def run_blocks(state_in, priors, flags, totals, block_states):
    running = state_in
    entering = []
    for number in range(flags.shape[0]):
        running = jnp.where(flags[number], priors[number], running)
        entering.append(running)
        running = totals[number][:, None, None] * running + block_states[number]
    return (jnp.stack(entering), running)


def nearest_first(place, count):
    return sorted(range(count), key=lambda j: (abs(j - place), j))


def tie(*values):
    return lax.optimization_barrier(values)


class Weights:
    def __init__(self, out_weight):
        self.count = lax.axis_size("seq")
        self.place = lax.axis_index("seq")
        self.halves = lax.axis_size("groups")
        part_cols = out_weight.shape[1] // lax.axis_size("batch")
        part_rows = out_weight.shape[0] // self.halves
        col = lax.axis_index("batch") * part_cols
        row = lax.axis_index("groups") * part_rows
        self.own = lax.dynamic_slice_in_dim(out_weight, col, part_cols, 1)
        self.own_half = lax.dynamic_slice(out_weight, (row, col), (part_rows, part_cols))
        self.up = self.down = self.own_half
        self.moved = {}
        self.arrivals = []

    def step(self):
        number = len(self.moved) // 2 + 1
        pairs = range(self.count - 1)
        self.up = lax.ppermute(self.up, "seq", [(i, i + 1) for i in pairs])
        self.down = lax.ppermute(self.down, "seq", [(i + 1, i) for i in pairs])
        self.moved[-number], self.moved[number] = self.up, self.down

    def settle(self, other):
        other, self.up, self.down = tie(other, self.up, self.down)
        number = len(self.moved) // 2
        self.moved[-number], self.moved[number] = self.up, self.down
        return other

    def choose(self, rank):
        chosen = None
        for offset in sorted(self.moved):
            places = [
                p for p in range(self.count) if nearest_first(p, self.count)[rank] - p == offset
            ]
            if not places:
                continue
            if chosen is None:
                chosen = self.moved[offset]
                continue
            here = functools.reduce(jnp.logical_or, [self.place == p for p in places])
            chosen = jnp.where(here, self.moved[offset], chosen)
        return chosen

    def swap(self, rank, other, pieces=1):
        other, chosen = tie(other, self.choose(rank))
        chosen = jnp.split(chosen, pieces, axis=1)
        n = self.halves
        self.arrivals.append(
            [
                [part]
                + [
                    lax.ppermute(part, "groups", [(i, (i + turn) % n) for i in range(n)])
                    for turn in range(1, n)
                ]
                for part in chosen
            ]
        )
        return other


def project(both_rows, weights, tokens):
    count, place, halves = weights.count, weights.place, weights.halves
    mine = lax.axis_index("groups")
    part_rows, part_cols = weights.own_half.shape
    strips = [
        lax.dynamic_slice_in_dim(
            both_rows, lax.rem(mine - turn + halves, halves) * part_rows, part_rows, 1
        )
        for turn in range(halves)
    ]
    orders = [nearest_first(p, count) for p in range(count)]
    ranks = [[order.index(j) for j in range(count)] for order in orders]
    rank_of = jnp.array(ranks, jnp.int32)[place]
    dot = functools.partial(jnp.dot, preferred_element_type=jnp.float32)
    def product(pieces):
        return sum(dot(strip, piece) for strip, piece in zip(strips, pieces)).astype(jnp.bfloat16)

    parts = [dot(both_rows, weights.own).astype(jnp.bfloat16)]
    parts += [product(arrival[0]) for arrival in weights.arrivals[:-1]]
    last = list(weights.arrivals[-1])
    parts, last[0] = tie(parts, last[0])
    cut = len(last)
    width = part_cols // cut
    pairs = lax.axis_size("batch")
    spans = count // lax.axis_size("head")
    sums = []
    for c in range(cut):
        ranked = jnp.stack([a[:, c * width : (c + 1) * width] for a in parts] + [product(last[c])])
        slots = jnp.concatenate(
            [lax.dynamic_slice_in_dim(ranked, rank_of[j], 1, 0) for j in range(count)]
        )
        sums.append(lax.psum_scatter(slots, "head", scatter_dimension=0, tiled=True))
    summed = jnp.concatenate(sums, axis=2)
    sections = summed.reshape(spans, pairs, tokens, part_cols)
    regrouped = lax.all_to_all(sections, "batch", split_axis=1, concat_axis=1, tiled=True)
    return jnp.transpose(regrouped, (2, 0, 1, 3)).reshape(1, tokens, spans * pairs * part_cols)


def chain(gain, state, weights):
    count, place = weights.count, weights.place
    cut = 2 if gain.shape[0] % 2 == 0 else 1
    gains, states = jnp.split(gain, cut), jnp.split(state, cut)
    entered = [jnp.zeros_like(a) for a in states]
    for hop in range(count - 1):
        for c in range(cut):
            leaving = (gains[c][:, None, None] * entered[c] + states[c]).astype(jnp.bfloat16)
            came = lax.ppermute(leaving, "seq", [(hop, hop + 1)])
            entered[c] = jnp.where(place == hop + 1, came.astype(jnp.float32), entered[c])
        if hop == 0:
            weights.step()
        else:
            entered[0] = weights.settle(entered[0])
            entered[0] = weights.swap(hop, entered[0])
            weights.step()
    return jnp.concatenate(entered)


def body(
    x_values,
    z_gate,
    write_basis,
    read_basis,
    step_size,
    log_decay,
    cached_states,
    session_slots,
    conv_lengths,
    norm_gain,
    out_weight,
):
    weights = Weights(out_weight)
    tokens = x_values.shape[1]
    width = x_values.shape[2]
    heads_dev = step_size.shape[2]
    groups_dev = write_basis.shape[2] // STATE
    per_group = heads_dev // groups_dev
    blocks = tokens // STRETCH
    seq_index = lax.axis_index("seq")
    block_ids = seq_index * blocks + jnp.arange(blocks, dtype=jnp.int32)
    lengths_row = conv_lengths[0]
    begins = jnp.cumsum(lengths_row) - lengths_row
    flags = jnp.any(begins[None, :] == block_ids[:, None], axis=1)
    owners = jnp.sum((begins[None, :] <= block_ids[:, None]).astype(jnp.int32), axis=1) - 1
    convs = jnp.arange(lengths_row.shape[0], dtype=jnp.int32)
    slot_ids = jnp.sum(
        jnp.where(convs[None, :] == owners[:, None], session_slots[0][None, :], 0), axis=1
    )
    picker = (convs[None, :] == slot_ids[:, None]).astype(jnp.bfloat16)
    chosen = jnp.einsum(
        "kc,chpn->khpn",
        picker,
        lax.all_gather(cached_states, "seq", axis=3, tiled=True)[0],
        preferred_element_type=jnp.float32,
    )
    values = x_values[0].reshape(blocks, STRETCH, heads_dev, HEAD_DIM)
    writes = write_basis[0].reshape(blocks, STRETCH, groups_dev, STATE)
    reads = read_basis[0].reshape(blocks, STRETCH, groups_dev, STATE)
    steps_b = step_size[0].reshape(blocks, STRETCH, heads_dev)
    logs = log_decay[0].reshape(blocks, STRETCH, heads_dev)
    running_log = jnp.cumsum(logs, axis=1)
    by_head = jnp.transpose(running_log, (0, 2, 1))
    lower = jnp.arange(STRETCH)[:, None] >= jnp.arange(STRETCH)[None, :]
    spread = by_head[:, :, :, None] - by_head[:, :, None, :]
    fading = jnp.where(lower, jnp.exp(jnp.where(lower, spread, 0.0)), 0.0)
    scores = jnp.einsum("cign,cjgn->cgij", reads, writes, preferred_element_type=jnp.float32)
    scores = jnp.repeat(scores, per_group, axis=1)
    mixing = (scores * fading * jnp.transpose(steps_b, (0, 2, 1))[:, :, None, :]).astype(
        jnp.bfloat16
    )
    inner = jnp.einsum("chij,cjhp->cihp", mixing, values, preferred_element_type=jnp.float32)
    to_end = jnp.exp(running_log[:, -1:, :] - running_log) * steps_b
    write_heads = jnp.repeat(writes, per_group, axis=2)
    weighted = (write_heads.astype(jnp.float32) * to_end[:, :, :, None]).astype(jnp.bfloat16)
    block_states = jnp.einsum(
        "cjhp,cjhn->chpn", values, weighted, preferred_element_type=jnp.float32
    )
    totals = jnp.exp(running_log[:, -1, :])
    whole_gain = jnp.prod(totals, axis=0) * (1.0 - jnp.any(flags).astype(jnp.float32))
    zero_state = jnp.zeros((heads_dev, HEAD_DIM, STATE), jnp.float32)
    unused, device_state = run_blocks(zero_state, chosen, flags, totals, block_states)
    state_in = chain(whole_gain, device_state, weights)
    early, late = weights.arrivals[:-1], weights.arrivals[-1:]
    state_in, early = tie(state_in, early)
    entering, unused_end = run_blocks(state_in, chosen, flags, totals, block_states)
    read_heads = jnp.repeat(reads, per_group, axis=2).astype(jnp.float32)
    inflow = jnp.exp(running_log)[:, :, :, None] * jnp.einsum(
        "cihn,chpn->cihp", read_heads, entering, precision=lax.Precision.HIGHEST
    )
    mixed = (inner + inflow).reshape(tokens, width)
    gated = mixed * jax.nn.silu(z_gate[0].astype(jnp.float32))
    grouped = gated.reshape(tokens, groups_dev, -1)
    scaled = grouped * lax.rsqrt(jnp.mean(grouped * grouped, axis=2, keepdims=True) + 1e-05)
    normed = (scaled.reshape(tokens, width) * norm_gain).astype(jnp.bfloat16)
    normed, late = tie(weights.settle(normed), late)
    weights.arrivals = early + late
    normed = weights.swap(weights.count - 1, normed, 2)
    both_rows = lax.all_gather(normed, "batch", axis=0, tiled=True)
    return project(both_rows, weights, tokens)


def solution(mesh):
    placed = (
        P(("groups", "batch"), "seq", "head"),
        P(("groups", "batch"), "seq", "head"),
        P(("groups", "batch"), "seq", "head"),
        P(("groups", "batch"), "seq", "head"),
        P(("groups", "batch"), "seq", "head"),
        P(("groups", "batch"), "seq", "head"),
        P(("groups", "batch"), None, "head", "seq", None),
        P(("groups", "batch"), None),
        P(("groups", "batch"), None),
        P("head"),
        P("head", "seq"),
    )
    return jax.shard_map(
        body,
        mesh=mesh,
        in_specs=placed,
        out_specs=P(("groups", "batch"), "seq", "head"),
        check_vma=False,
    )
```

```python
import functools

import jax
import jax.numpy as jnp
from jax import lax
from jax.sharding import PartitionSpec as P

HEAD_DIM = 64
STATE = 128
STRETCH = 128


def run_blocks(state_in, priors, flags, totals, block_states):
    running = state_in
    entering = []
    for number in range(flags.shape[0]):
        running = jnp.where(flags[number], priors[number], running)
        entering.append(running)
        running = totals[number][:, None, None] * running + block_states[number]
    return (jnp.stack(entering), running)


def nearest_first(place, count):
    return sorted(range(count), key=lambda j: (abs(j - place), j))


def tie(*values):
    return lax.optimization_barrier(values)


class Weights:
    def __init__(self, out_weight):
        self.count = lax.axis_size("seq")
        self.place = lax.axis_index("seq")
        self.halves = lax.axis_size("groups")
        part_cols = out_weight.shape[1] // lax.axis_size("batch")
        part_rows = out_weight.shape[0] // self.halves
        col = lax.axis_index("batch") * part_cols
        row = lax.axis_index("groups") * part_rows
        self.own = lax.dynamic_slice_in_dim(out_weight, col, part_cols, 1)
        self.own_half = lax.dynamic_slice(out_weight, (row, col), (part_rows, part_cols))
        orders = [nearest_first(p, self.count) for p in range(self.count)]
        ranks = [[order.index(j) for j in range(self.count)] for order in orders]
        self.rank_of, self.own_half = tie(
            jnp.array(ranks, jnp.int32)[self.place], self.own_half
        )
        self.up = self.down = self.own_half
        self.cut = 2
        self.steps = 0
        self.moved = {}
        self.arrivals = []

    def step(self):
        number = self.steps = self.steps + 1
        pairs = range(self.count - 1)
        self.moved[-number] = [lax.ppermute(self.up, "seq", [(i, i + 1) for i in pairs])]
        self.moved[number] = [lax.ppermute(self.down, "seq", [(i + 1, i) for i in pairs])]

    def settle(self, other, piece=0):
        number = self.steps
        up, down = self.moved[-number], self.moved[number]
        other, up[piece], down[piece] = tie(other, up[piece], down[piece])
        self.up, self.down = up[piece], down[piece]
        return other

    def pick(self, offset, piece, cut):
        found = self.moved[offset]
        if len(found) == cut:
            return found[piece]
        return jnp.split(found[0], cut, axis=1)[piece]

    def swap(self, rank, other, piece=0, cut=1):
        chosen = None
        for offset in sorted(self.moved):
            places = [
                p for p in range(self.count) if nearest_first(p, self.count)[rank] - p == offset
            ]
            if not places:
                continue
            candidate = self.pick(offset, piece, cut)
            if chosen is None:
                chosen = candidate
                continue
            here = functools.reduce(jnp.logical_or, [self.place == p for p in places])
            chosen = jnp.where(here, candidate, chosen)
        other, chosen = tie(other, chosen)
        n = self.halves
        swapped = [
            lax.ppermute(chosen, "groups", [(i, (i + turn) % n) for i in range(n)])
            for turn in range(1, n)
        ]
        return other, [chosen] + swapped


def project(both_rows, weights, tokens):
    count, place, halves = weights.count, weights.place, weights.halves
    mine = lax.axis_index("groups")
    part_rows, part_cols = weights.own_half.shape
    strips = [
        lax.dynamic_slice_in_dim(
            both_rows, lax.rem(mine - turn + halves, halves) * part_rows, part_rows, 1
        )
        for turn in range(halves)
    ]
    rank_of = weights.rank_of
    dot = functools.partial(jnp.dot, preferred_element_type=jnp.float32)
    def product(pieces):
        return sum(dot(strip, piece) for strip, piece in zip(strips, pieces)).astype(jnp.bfloat16)

    cut, rank = weights.cut, count - 1
    last = []
    both_rows = weights.settle(both_rows)
    for c in range(cut):
        both_rows, piece = weights.swap(rank, both_rows, c, cut)
        last.append(piece)
    both_rows, weights.arrivals = tie(both_rows, weights.arrivals)
    parts = [dot(both_rows, weights.own).astype(jnp.bfloat16)]
    parts += [product(arrival) for arrival in weights.arrivals[:1]]
    parts += [product(arrival) for arrival in weights.arrivals[1:]]
    parts, last[0] = tie(parts, last[0])
    width = part_cols // cut
    pairs = lax.axis_size("batch")
    spans = count // lax.axis_size("head")
    sums = []
    for c in range(cut):
        ranked = jnp.stack([a[:, c * width : (c + 1) * width] for a in parts] + [product(last[c])])
        slots = jnp.concatenate(
            [lax.dynamic_slice_in_dim(ranked, rank_of[j], 1, 0) for j in range(count)]
        )
        sums.append(lax.psum_scatter(slots, "head", scatter_dimension=0, tiled=True))
    summed = jnp.concatenate(sums, axis=2)
    sections = summed.reshape(spans, pairs, tokens, part_cols)
    regrouped = lax.all_to_all(sections, "batch", split_axis=1, concat_axis=1, tiled=True)
    return jnp.transpose(regrouped, (2, 0, 1, 3)).reshape(1, tokens, spans * pairs * part_cols)


def advance(weights, held, rank):
    held[0] = weights.settle(held[0])
    held[0], arrival = weights.swap(rank, held[0])
    weights.arrivals.append(arrival)
    weights.step()


def chain(gain, state, weights):
    count, place = weights.count, weights.place
    cut = 2 if gain.shape[0] % 2 == 0 else 1
    gains, states = jnp.split(gain, cut), jnp.split(state, cut)
    entered = [jnp.zeros_like(a) for a in states]
    for hop in range(count - 1):
        for c in range(cut):
            leaving = (gains[c][:, None, None] * entered[c] + states[c]).astype(jnp.bfloat16)
            came = lax.ppermute(leaving, "seq", [(hop, hop + 1)])
            entered[c] = jnp.where(place == hop + 1, came.astype(jnp.float32), entered[c])
        if 0 < hop < count - 2:
            advance(weights, entered, hop)
    return jnp.concatenate(entered)


def body(
    x_values,
    z_gate,
    write_basis,
    read_basis,
    step_size,
    log_decay,
    cached_states,
    session_slots,
    conv_lengths,
    norm_gain,
    out_weight,
):
    weights = Weights(out_weight)
    tokens = x_values.shape[1]
    width = x_values.shape[2]
    heads_dev = step_size.shape[2]
    groups_dev = write_basis.shape[2] // STATE
    per_group = heads_dev // groups_dev
    blocks = tokens // STRETCH
    seq_index = lax.axis_index("seq")
    block_ids = seq_index * blocks + jnp.arange(blocks, dtype=jnp.int32)
    lengths_row = conv_lengths[0]
    begins = jnp.cumsum(lengths_row) - lengths_row
    flags = jnp.any(begins[None, :] == block_ids[:, None], axis=1)
    owners = jnp.sum((begins[None, :] <= block_ids[:, None]).astype(jnp.int32), axis=1) - 1
    convs = jnp.arange(lengths_row.shape[0], dtype=jnp.int32)
    slot_ids = jnp.sum(
        jnp.where(convs[None, :] == owners[:, None], session_slots[0][None, :], 0), axis=1
    )
    picker = (convs[None, :] == slot_ids[:, None]).astype(jnp.bfloat16)
    chosen = jnp.einsum(
        "kc,chpn->khpn",
        picker,
        lax.all_gather(cached_states, "seq", axis=3, tiled=True)[0],
        preferred_element_type=jnp.float32,
    )
    values = x_values[0].reshape(blocks, STRETCH, heads_dev, HEAD_DIM)
    writes = write_basis[0].reshape(blocks, STRETCH, groups_dev, STATE)
    reads = read_basis[0].reshape(blocks, STRETCH, groups_dev, STATE)
    steps_b = step_size[0].reshape(blocks, STRETCH, heads_dev)
    logs = log_decay[0].reshape(blocks, STRETCH, heads_dev)
    running_log = jnp.cumsum(logs, axis=1)
    by_head = jnp.transpose(running_log, (0, 2, 1))
    lower = jnp.arange(STRETCH)[:, None] >= jnp.arange(STRETCH)[None, :]
    spread = by_head[:, :, :, None] - by_head[:, :, None, :]
    fading = jnp.where(lower, jnp.exp(jnp.where(lower, spread, 0.0)), 0.0)
    scores = jnp.einsum("cign,cjgn->cgij", reads, writes, preferred_element_type=jnp.float32)
    scores = jnp.repeat(scores, per_group, axis=1)
    mixing = (scores * fading * jnp.transpose(steps_b, (0, 2, 1))[:, :, None, :]).astype(
        jnp.bfloat16
    )
    inner = jnp.einsum("chij,cjhp->cihp", mixing, values, preferred_element_type=jnp.float32)
    to_end = jnp.exp(running_log[:, -1:, :] - running_log) * steps_b
    write_heads = jnp.repeat(writes, per_group, axis=2)
    weighted = (write_heads.astype(jnp.float32) * to_end[:, :, :, None]).astype(jnp.bfloat16)
    block_states = jnp.einsum(
        "cjhp,cjhn->chpn", values, weighted, preferred_element_type=jnp.float32
    )
    totals = jnp.exp(running_log[:, -1, :])
    whole_gain = jnp.prod(totals, axis=0) * (1.0 - jnp.any(flags).astype(jnp.float32))
    zero_state = jnp.zeros((heads_dev, HEAD_DIM, STATE), jnp.float32)
    chosen, weights.up = tie(chosen, weights.up)
    weights.down = weights.up
    unused, device_state = run_blocks(zero_state, chosen, flags, totals, block_states)
    weights.step()
    state_in = chain(whole_gain, device_state, weights)
    entering, unused_end = run_blocks(state_in, chosen, flags, totals, block_states)
    read_heads = jnp.repeat(reads, per_group, axis=2).astype(jnp.float32)
    inflow = jnp.exp(running_log)[:, :, :, None] * jnp.einsum(
        "cihn,chpn->cihp", read_heads, entering, precision=lax.Precision.HIGHEST
    )
    mixed = (inner + inflow).reshape(tokens, width)
    mixed, weights.arrivals = tie(mixed, weights.arrivals)
    held = [mixed]
    advance(weights, held, weights.steps)
    mixed = held[0]
    gated = mixed * jax.nn.silu(z_gate[0].astype(jnp.float32))
    grouped = gated.reshape(tokens, groups_dev, -1)
    scaled = grouped * lax.rsqrt(jnp.mean(grouped * grouped, axis=2, keepdims=True) + 1e-05)
    normed = (scaled.reshape(tokens, width) * norm_gain).astype(jnp.bfloat16)
    both_rows = lax.all_gather(normed, "batch", axis=0, tiled=True)
    return project(both_rows, weights, tokens)


def solution(mesh):
    placed = (
        P(("groups", "batch"), "seq", "head"),
        P(("groups", "batch"), "seq", "head"),
        P(("groups", "batch"), "seq", "head"),
        P(("groups", "batch"), "seq", "head"),
        P(("groups", "batch"), "seq", "head"),
        P(("groups", "batch"), "seq", "head"),
        P(("groups", "batch"), None, "head", "seq", None),
        P(("groups", "batch"), None),
        P(("groups", "batch"), None),
        P("head"),
        P("head", "seq"),
    )
    return jax.shard_map(
        body,
        mesh=mesh,
        in_specs=placed,
        out_specs=P(("groups", "batch"), "seq", "head"),
        check_vma=False,
    )
```

```python
import functools

import jax
import jax.numpy as jnp
from jax import lax
from jax.sharding import PartitionSpec as P

HEAD_DIM = 64
STATE = 128
STRETCH = 128


def run_blocks(state_in, priors, flags, totals, block_states):
    running = state_in
    entering = []
    for number in range(flags.shape[0]):
        running = jnp.where(flags[number], priors[number], running)
        entering.append(running)
        running = totals[number][:, None, None] * running + block_states[number]
    return (jnp.stack(entering), running)


def nearest_first(place, count):
    return sorted(range(count), key=lambda j: (abs(j - place), j))


def tie(*values):
    return lax.optimization_barrier(values)


class Weights:
    def __init__(self, out_weight):
        self.count = lax.axis_size("seq")
        self.place = lax.axis_index("seq")
        self.halves = lax.axis_size("groups")
        part_cols = out_weight.shape[1] // lax.axis_size("batch")
        part_rows = out_weight.shape[0] // self.halves
        col = lax.axis_index("batch") * part_cols
        row = lax.axis_index("groups") * part_rows
        self.own = lax.dynamic_slice_in_dim(out_weight, col, part_cols, 1)
        self.own_half = lax.dynamic_slice(out_weight, (row, col), (part_rows, part_cols))
        orders = [nearest_first(p, self.count) for p in range(self.count)]
        ranks = [[order.index(j) for j in range(self.count)] for order in orders]
        self.rank_of, self.own_half = tie(
            jnp.array(ranks, jnp.int32)[self.place], self.own_half
        )
        self.up = self.down = self.own_half
        self.steps = 0
        self.moved = {}
        self.arrivals = []

    def step(self):
        number = self.steps = self.steps + 1
        pairs = range(self.count - 1)
        self.moved[-number] = [lax.ppermute(self.up, "seq", [(i, i + 1) for i in pairs])]
        self.moved[number] = [lax.ppermute(self.down, "seq", [(i + 1, i) for i in pairs])]

    def settle(self, other, piece=0):
        number = self.steps
        up, down = self.moved[-number], self.moved[number]
        other, up[piece], down[piece] = tie(other, up[piece], down[piece])
        self.up, self.down = up[piece], down[piece]
        return other

    def pick(self, offset, piece, cut):
        found = self.moved[offset]
        if len(found) == cut:
            return found[piece]
        return jnp.split(found[0], cut, axis=1)[piece]

    def swap(self, rank, other, piece=0, cut=1):
        chosen = None
        for offset in sorted(self.moved):
            places = [
                p for p in range(self.count) if nearest_first(p, self.count)[rank] - p == offset
            ]
            if not places:
                continue
            candidate = self.pick(offset, piece, cut)
            if chosen is None:
                chosen = candidate
                continue
            here = functools.reduce(jnp.logical_or, [self.place == p for p in places])
            chosen = jnp.where(here, candidate, chosen)
        other, chosen = tie(other, chosen)
        n = self.halves
        swapped = [
            lax.ppermute(chosen, "groups", [(i, (i + turn) % n) for i in range(n)])
            for turn in range(1, n)
        ]
        return other, [chosen] + swapped


def project(both_rows, weights, tokens):
    count, place, halves = weights.count, weights.place, weights.halves
    mine = lax.axis_index("groups")
    part_rows, part_cols = weights.own_half.shape
    strips = [
        lax.dynamic_slice_in_dim(
            both_rows, lax.rem(mine - turn + halves, halves) * part_rows, part_rows, 1
        )
        for turn in range(halves)
    ]
    rank_of = weights.rank_of
    dot = functools.partial(jnp.dot, preferred_element_type=jnp.float32)
    def product(pieces):
        return sum(dot(strip, piece) for strip, piece in zip(strips, pieces)).astype(jnp.bfloat16)

    parts = [dot(both_rows, weights.own).astype(jnp.bfloat16)]
    parts += [product(arrival) for arrival in weights.arrivals]
    pairs = lax.axis_size("batch")
    spans = count // lax.axis_size("head")
    ranked = jnp.stack(parts)
    slots = jnp.concatenate(
        [lax.dynamic_slice_in_dim(ranked, rank_of[j], 1, 0) for j in range(count)]
    )
    summed = lax.psum_scatter(slots, "head", scatter_dimension=0, tiled=True)
    sections = summed.reshape(spans, pairs, tokens, part_cols)
    regrouped = lax.all_to_all(sections, "batch", split_axis=1, concat_axis=1, tiled=True)
    return jnp.transpose(regrouped, (2, 0, 1, 3)).reshape(1, tokens, spans * pairs * part_cols)


def advance(weights, held, rank):
    held[0] = weights.settle(held[0])
    held[0], arrival = weights.swap(rank, held[0])
    weights.arrivals.append(arrival)
    weights.step()


def chain(gain, state, weights):
    count, place = weights.count, weights.place
    cut = 2 if gain.shape[0] % 2 == 0 else 1
    gains, states = jnp.split(gain, cut), jnp.split(state, cut)
    entered = [jnp.zeros_like(a) for a in states]
    for hop in range(count - 1):
        for c in range(cut):
            leaving = (gains[c][:, None, None] * entered[c] + states[c]).astype(jnp.bfloat16)
            came = lax.ppermute(leaving, "seq", [(hop, hop + 1)])
            entered[c] = jnp.where(place == hop + 1, came.astype(jnp.float32), entered[c])
        if hop < count - 2:
            advance(weights, entered, hop + 1)
    return jnp.concatenate(entered)


def body(
    x_values,
    z_gate,
    write_basis,
    read_basis,
    step_size,
    log_decay,
    cached_states,
    session_slots,
    conv_lengths,
    norm_gain,
    out_weight,
):
    weights = Weights(out_weight)
    weights.step()
    tokens = x_values.shape[1]
    width = x_values.shape[2]
    heads_dev = step_size.shape[2]
    groups_dev = write_basis.shape[2] // STATE
    per_group = heads_dev // groups_dev
    blocks = tokens // STRETCH
    seq_index = lax.axis_index("seq")
    block_ids = seq_index * blocks + jnp.arange(blocks, dtype=jnp.int32)
    lengths_row = conv_lengths[0]
    begins = jnp.cumsum(lengths_row) - lengths_row
    flags = jnp.any(begins[None, :] == block_ids[:, None], axis=1)
    owners = jnp.sum((begins[None, :] <= block_ids[:, None]).astype(jnp.int32), axis=1) - 1
    convs = jnp.arange(lengths_row.shape[0], dtype=jnp.int32)
    slot_ids = jnp.sum(
        jnp.where(convs[None, :] == owners[:, None], session_slots[0][None, :], 0), axis=1
    )
    picker = (convs[None, :] == slot_ids[:, None]).astype(jnp.bfloat16)
    chosen = jnp.einsum(
        "kc,chpn->khpn",
        picker,
        lax.all_gather(cached_states, "seq", axis=3, tiled=True)[0],
        preferred_element_type=jnp.float32,
    )
    values = x_values[0].reshape(blocks, STRETCH, heads_dev, HEAD_DIM)
    writes = write_basis[0].reshape(blocks, STRETCH, groups_dev, STATE)
    reads = read_basis[0].reshape(blocks, STRETCH, groups_dev, STATE)
    steps_b = step_size[0].reshape(blocks, STRETCH, heads_dev)
    logs = log_decay[0].reshape(blocks, STRETCH, heads_dev)
    running_log = jnp.cumsum(logs, axis=1)
    by_head = jnp.transpose(running_log, (0, 2, 1))
    lower = jnp.arange(STRETCH)[:, None] >= jnp.arange(STRETCH)[None, :]
    spread = by_head[:, :, :, None] - by_head[:, :, None, :]
    fading = jnp.where(lower, jnp.exp(jnp.where(lower, spread, 0.0)), 0.0)
    scores = jnp.einsum("cign,cjgn->cgij", reads, writes, preferred_element_type=jnp.float32)
    scores = jnp.repeat(scores, per_group, axis=1)
    mixing = (scores * fading * jnp.transpose(steps_b, (0, 2, 1))[:, :, None, :]).astype(
        jnp.bfloat16
    )
    inner = jnp.einsum("chij,cjhp->cihp", mixing, values, preferred_element_type=jnp.float32)
    to_end = jnp.exp(running_log[:, -1:, :] - running_log) * steps_b
    write_heads = jnp.repeat(writes, per_group, axis=2)
    weighted = (write_heads.astype(jnp.float32) * to_end[:, :, :, None]).astype(jnp.bfloat16)
    block_states = jnp.einsum(
        "cjhp,cjhn->chpn", values, weighted, preferred_element_type=jnp.float32
    )
    totals = jnp.exp(running_log[:, -1, :])
    whole_gain = jnp.prod(totals, axis=0) * (1.0 - jnp.any(flags).astype(jnp.float32))
    zero_state = jnp.zeros((heads_dev, HEAD_DIM, STATE), jnp.float32)
    unused, device_state = run_blocks(zero_state, chosen, flags, totals, block_states)
    state_in = weights.settle(chain(whole_gain, device_state, weights))
    early = weights.arrivals
    state_in, early[:1] = tie(state_in, early[:1])
    state_in, final = weights.swap(weights.count - 1, state_in)
    entering, unused_end = run_blocks(state_in, chosen, flags, totals, block_states)
    read_heads = jnp.repeat(reads, per_group, axis=2).astype(jnp.float32)
    inflow = jnp.exp(running_log)[:, :, :, None] * jnp.einsum(
        "cihn,chpn->cihp", read_heads, entering, precision=lax.Precision.HIGHEST
    )
    mixed = (inner + inflow).reshape(tokens, width)
    mixed, early = tie(mixed, early)
    gated = mixed * jax.nn.silu(z_gate[0].astype(jnp.float32))
    grouped = gated.reshape(tokens, groups_dev, -1)
    scaled = grouped * lax.rsqrt(jnp.mean(grouped * grouped, axis=2, keepdims=True) + 1e-05)
    normed = (scaled.reshape(tokens, width) * norm_gain).astype(jnp.bfloat16)
    normed, final = tie(normed, final)
    weights.arrivals = early + [final]
    both_rows = lax.all_gather(normed, "batch", axis=0, tiled=True)
    return project(both_rows, weights, tokens)


def solution(mesh):
    placed = (
        P(("groups", "batch"), "seq", "head"),
        P(("groups", "batch"), "seq", "head"),
        P(("groups", "batch"), "seq", "head"),
        P(("groups", "batch"), "seq", "head"),
        P(("groups", "batch"), "seq", "head"),
        P(("groups", "batch"), "seq", "head"),
        P(("groups", "batch"), None, "head", "seq", None),
        P(("groups", "batch"), None),
        P(("groups", "batch"), None),
        P("head"),
        P("head", "seq"),
    )
    return jax.shard_map(
        body,
        mesh=mesh,
        in_specs=placed,
        out_specs=P(("groups", "batch"), "seq", "head"),
        check_vma=False,
    )
```
